32 devices in a mesh: grp: 2 (over y), gx: 4 (over z), gy: 2 (over x), row: 2 (over core).
Axes of the slice: x: 2, y: 2, z: 4, core: 2. Of those that a mesh axis runs over, the one named last changes fastest.
Arguments:
- conc: float32 [64, 8, 16, 128], P(None, ('grp', 'gx'), ('gy', 'row')), parts along dimension 1, may hold values from 0.2 to 2
- cotangent: float32 [64, 8, 16, 128], P(None, ('grp', 'gx'), ('gy', 'row')), parts along dimension 1, may hold values from -6 to 6
- courant: float32 [32, 128], P(('grp', 'gy', 'row')), parts along dimension 0, may hold values from 8 to 100
- direction: int32 [32, 128], P(('grp', 'gy', 'row')), parts along dimension 0, may hold values 0 or 1
- rate_const: float32 [1024], replicated, may hold values from 0.01 to 0.1
- orders: int32 [1024, 64], replicated, may hold values from 0 to 2, as said below
- stoich: int32 [64, 1024], replicated, may hold values from -2 to 1, as said below
Outputs:
- final_state: float32 [64, 8, 16, 128], P(None, ('grp', 'gx'), ('gy', 'row')), parts along dimension 1
- adjoint: float32 [64, 8, 16, 128], P(None, ('grp', 'gx'), ('gy', 'row')), parts along dimension 1
The draws below stay inside these ranges and needn't reach their ends.
There are 2 independent parts, one for each index of `grp`. The reference program is written for one: setup_inputs(seed, part) draws one part's arguments, and reference() takes and returns one part's arrays. A program takes and returns all parts, laid end to end along the dimension named above; an argument that names none is the same for every part. Nothing has to cross between parts.
Inputs may be any that keep to these rules, and one draw needn't show every extreme that they name: `orders`: each reaction has two different reactants, each of order 1 or 2, and no other nonzero order. stoich[s, j] is 1 for the product species of reaction j (one species) minus orders[j, s].
All inputs are finite; a program needn't handle non-finite values. No bound on the sum of `direction` on one device may be relied on, other than what follows from the above.
Results may differ from the reference program's by a relative error of at most 0.0003.
Values sent between devices are 32-bit elements; how exact they have to be, the bound alone decides.
No kernel may reach another device: no remote copies, remote signals or barrier semaphores. Data moves between devices by JAX's collectives and lax.ppermute only.
A program may use at most 64 MiB of HBM per device.

```python
import math
import jax
import jax.numpy as jnp
from jax import lax

S = 64
R = 1024
NZ = 128
STEPS = 2
NX = 4
NY = 16


def reaction_table(key):
    base = jax.random.fold_in(key, 11)
    key_one, key_two, key_three, key_four, key_five = jax.random.split(base, 5)
    reactant_one = jax.random.randint(key_one, (R,), 0, S)
    reactant_two = (reactant_one + jax.random.randint(key_two, (R,), 1, S)) % S
    product = jax.random.randint(key_three, (R,), 0, S)
    order_one = jax.random.randint(key_four, (R,), 1, 3)
    order_two = jax.random.randint(key_five, (R,), 1, 3)
    species = jnp.arange(S, dtype=jnp.int32)[None, :]
    orders = (species == reactant_one[:, None]).astype(jnp.int32) * order_one[:, None]
    orders = orders + (species == reactant_two[:, None]).astype(jnp.int32) * order_two[:, None]
    stoich = (species == product[:, None]).astype(jnp.int32) - orders
    return (orders, stoich.T)


def draw_orders(key, part):
    return reaction_table(key)[0]


def draw_stoich(key, part):
    return reaction_table(key)[1]


def touch_ends(entries, rng, smallest, largest):
    spot = [jax.random.randint(jax.random.fold_in(rng, axis), (), 0, length) for axis, length in enumerate(entries.shape)]
    main_axis = entries.shape.index(max(entries.shape))
    beside = spot[:main_axis] + [(spot[main_axis] + 1) % entries.shape[main_axis]] + spot[main_axis + 1:]
    return entries.at[tuple(spot)].set(smallest).at[tuple(beside)].set(largest)


def steps_of(rng, shape, cuts, least, high):
    level, own = 1.0, jax.random.fold_in(rng, 6)
    for axis_at, shards_of in cuts:
        heights = jnp.exp(jax.random.uniform(jax.random.fold_in(own, axis_at), (shards_of,), jnp.float32, least / len(cuts), high / len(cuts)))
        level = level * jnp.repeat(heights, shape[axis_at] // shards_of).reshape([-1 if axis == axis_at else 1 for axis in range(len(shape))])
    return level


def gaussian(key, dims, width, bound, cuts=(), kind=jnp.bfloat16):
    loudness = steps_of(key, dims, cuts, -0.22, 0.18) if cuts else 1.0
    entries = jax.random.normal(key, dims, jnp.float32) * width * loudness
    return jnp.minimum(jnp.maximum(entries, -bound), bound).astype(kind)


def setup_inputs(seed: int = 0, part: int = 0) -> dict:
    key_list = jax.random.split(jax.random.key(seed), 8)
    part_keys = jax.random.split(jax.random.fold_in(key_list[7], part), 8)
    conc = jnp.clip(0.2 + 1.8 * jax.random.uniform(part_keys[0], (S, NX, NY, NZ), jnp.float32) ** steps_of(part_keys[0], (S, NX, NY, NZ), ((1, 4), (2, 4)), -0.2, 0.2), 0.2, 2.0)
    cotangent = gaussian(part_keys[1], (S, NX, NY, NZ), 1.0, 6.0, ((1, 4), (2, 4)), jnp.float32)
    courant = jnp.clip(jnp.exp(math.log(100.0) - 2.5257286 * jax.random.uniform(part_keys[2], (NY, NZ), jnp.float32) ** steps_of(part_keys[2], (NY, NZ), ((0, 4),), -0.2, 0.2)), 8.0, 100.0)
    direction = touch_ends((jax.random.randint(part_keys[3], (NY, NZ), 0, 2) < 1).astype(jnp.int32), jax.random.fold_in(part_keys[3], 1), 0, 1)
    rate_const = jnp.clip(jnp.exp(jax.random.uniform(key_list[4], (R,), jnp.float32, math.log(0.01), math.log(0.1))), 0.01, 0.1)
    orders = draw_orders(jax.random.fold_in(key_list[7], 71), part)
    stoich = draw_stoich(jax.random.fold_in(key_list[7], 71), part)
    return dict(conc=conc, cotangent=cotangent, courant=courant, direction=direction, rate_const=rate_const, orders=orders, stoich=stoich)


time_step = 0.1
diffusion = 0.1
highest = lax.Precision.HIGHEST


def combine_pairs(leading, trailing):
    return (leading[0] * trailing[0], trailing[0] * leading[1] + trailing[1])


def recurrence(values, weight, backward):
    multipliers = jnp.broadcast_to(weight[None, None], (1, values.shape[1]) + weight.shape)
    return lax.associative_scan(combine_pairs, (multipliers, values), reverse=backward, axis=1)


def sweep(values, weight, upward):
    rising = recurrence(values, weight, False)[1]
    falling = recurrence(values, weight, True)[1]
    return jnp.where(upward[None, None], rising, falling)


def smooth(values):
    padded = jnp.pad(values, ((0, 0), (0, 0), (1, 1), (1, 1)))
    beside_all = padded[:, :, 2:, 1:-1] + padded[:, :, :-2, 1:-1] + padded[:, :, 1:-1, 2:] + padded[:, :, 1:-1, :-2]
    return values + diffusion * (beside_all - 4.0 * values)


def to_slices(values):
    return jnp.moveaxis(values.reshape(values.shape[0], values.shape[1], -1), 1, 0)


def from_slices(slices, shape):
    return jnp.moveaxis(slices, 0, 1).reshape(shape)


def reaction_rates(cells, order_float, rate_const):
    activity = 0.5 * jnp.log1p(cells * cells)
    return rate_const[:, None] * jnp.exp(jnp.dot(order_float, activity, precision=highest))


def reference(conc, cotangent, courant, direction, rate_const, orders, stoich):
    order_float = orders.astype(jnp.float32)
    stoich_float = stoich.astype(jnp.float32)
    retain = courant / (1.0 + courant)
    admit = 1.0 / (1.0 + courant)

    def react(cells):
        return cells + time_step * jnp.dot(stoich_float, reaction_rates(cells, order_float, rate_const), precision=highest)

    def react_back(paired):
        cells, spread = paired
        rates = reaction_rates(cells, order_float, rate_const)
        pulled = jnp.dot(stoich_float.T, spread, precision=highest)
        summed = jnp.dot(order_float.T, rates * pulled, precision=highest)
        return spread + time_step * cells / (1.0 + cells * cells) * summed

    states = [conc]
    for position in range(STEPS):
        current = states[-1]
        starred = from_slices(lax.map(react, to_slices(current)), current.shape)
        states.append(sweep(admit * smooth(starred), retain, direction == 1))
    adjoint = cotangent
    for position in reversed(range(STEPS)):
        carried = admit * sweep(adjoint, retain, direction == 0)
        spread = smooth(carried)
        adjoint = from_slices(lax.map(react_back, (to_slices(states[position]), to_slices(spread))), spread.shape)
    return states[-1], adjoint
```

```python
import functools
import jax
import jax.numpy as jnp
from jax import lax
from jax.experimental import pallas as pl
from jax.experimental.pallas import tpu as pltpu
from jax.sharding import PartitionSpec as P

STEPS = 2
LANES = 128

time_step = 0.1
diffusion = 0.1
highest = lax.Precision.HIGHEST
f32 = jnp.float32
bf16 = jnp.bfloat16


def padded_2(block, sides, width):
    for axis, dim in sides:
        count = lax.axis_size(axis)
        forward = [(i, i + 1) for i in range(count - 1)]
        backward = [(target, source) for source, target in forward]
        low = lax.ppermute(
            lax.slice_in_dim(block, block.shape[dim] - width, None, axis=dim), axis, forward
        )
        high = lax.ppermute(lax.slice_in_dim(block, 0, width, axis=dim), axis, backward)
        block = jnp.concatenate([low, block, high], axis=dim)
    return block


def combine_pairs(leading, trailing):
    return (leading[0] * trailing[0], trailing[0] * leading[1] + trailing[1])


def recurrence(values, weight, backward):
    multipliers = jnp.broadcast_to(weight[None, None], (1, values.shape[1]) + weight.shape)
    return lax.associative_scan(combine_pairs, (multipliers, values), reverse=backward, axis=1)


def sweep(values, weight, upward):
    pencils = lax.all_to_all(values, "gx", split_axis=0, concat_axis=1, tiled=True)
    rising = recurrence(pencils, weight, False)[1]
    falling = recurrence(pencils, weight, True)[1]
    result = jnp.where(upward[None, None], rising, falling)
    return lax.all_to_all(result, "gx", split_axis=1, concat_axis=0, tiled=True)


def smooth(values):
    padded = padded_2(values, ((("gy", "row"), 2),), 1)
    padded = jnp.pad(padded, [(0, 0)] * (padded.ndim - 1) + [(1, 1)])
    beside_all = (
        padded[..., 2:, 1:-1]
        + padded[..., :-2, 1:-1]
        + padded[..., 1:-1, 2:]
        + padded[..., 1:-1, :-2]
    )
    return values + diffusion * (beside_all - 4.0 * values)


def reaction_rates(cells, order_float, rate_const):
    activity = 0.5 * jnp.log1p(cells * cells)
    return rate_const[:, None] * jnp.exp(jnp.dot(order_float, activity, precision=highest))


def per_slice(function, arrays, shape):
    flats = [item.reshape(shape[0], -1) for item in arrays]
    return function(*flats).reshape(shape)


def general(conc, cotangent, courant, direction, rate_const, orders, stoich):
    order_float = orders.astype(f32)
    stoich_float = stoich.astype(f32)
    order_trans = order_float.T
    stoich_trans = stoich_float.T
    retain = courant / (1.0 + courant)
    admit = 1.0 / (1.0 + courant)

    def react(cells):
        return cells + time_step * jnp.dot(
            stoich_float, reaction_rates(cells, order_float, rate_const), precision=highest
        )

    def react_back(cells, spread):
        rates = reaction_rates(cells, order_float, rate_const)
        pulled = jnp.dot(stoich_trans, spread, precision=highest)
        summed = jnp.dot(order_trans, rates * pulled, precision=highest)
        return spread + time_step * cells / (1.0 + cells * cells) * summed

    states = [conc]
    for position in range(STEPS):
        current = states[-1]
        starred = per_slice(react, [current], current.shape)
        states.append(sweep(admit * smooth(starred), retain, direction == 1))
    adjoint = cotangent
    for position in reversed(range(STEPS)):
        carried = admit * sweep(adjoint, retain, direction == 0)
        spread = smooth(carried)
        adjoint = per_slice(react_back, [states[position], spread], spread.shape)
    return (states[-1], adjoint)


def split(values):
    high = values.astype(bf16)
    return high, (values - high.astype(f32)).astype(bf16)


def stacked(values):
    high, low = split(values)
    return jnp.concatenate([high, low], axis=0)


def mul(left, right):
    return jnp.dot(left, right, preferred_element_type=f32)


def exponent_input(cells):
    return stacked((0.5 * 1.4426950408889634) * jnp.log(1.0 + cells * cells))


def scaled(left, rate_const):
    return stacked(left * rate_const)


def product(left, values):
    species = left.shape[0] // 2
    high, low = split(values)
    both = mul(left, high)
    return both[:species] + both[species:] + mul(left[:species], low)


def lane_iota(rows):
    return lax.broadcasted_iota(jnp.int32, (rows, LANES), 1)


class Plan:
    def __init__(self, species, rows, depth, parts):
        self.species, self.rows, self.depth, self.parts = species, rows, depth, parts
        self.halo = STEPS
        self.cut = depth // parts
        self.width = self.cut + 2 * self.halo
        self.own = rows * self.width
        self.tail = self.own - LANES
        self.groups = LANES // self.tail if self.tail > 0 and LANES % self.tail == 0 else 0
        need = (rows + 2 * self.halo) * self.width
        self.lanes = -(-need // LANES) * LANES
        need = (rows + 2 * self.halo - 2) * self.width
        self.inner = -(-need // LANES) * LANES


def fits(mesh, conc):
    parts = mesh.shape["gx"]
    species, length, across, depth = conc
    rows = across // (mesh.shape["gy"] * mesh.shape["row"])
    if mesh.shape["row"] != 2 or length != mesh.shape["grp"] * parts or depth != LANES:
        return False
    if depth % parts or parts not in (2, 4, 8) or rows != parts or STEPS != 2:
        return False
    plan = Plan(species, rows, depth, parts)
    if plan.groups == 0 or (2 * species) % (8 * plan.groups) or species % 16:
        return False
    if (rows - 1) * plan.width >= LANES or plan.tail + 2 * plan.width > LANES:
        return False
    return plan.lanes >= 3 * LANES


def window(pieces, target, plan):
    count = pieces[0].shape[0]
    lane = lane_iota(count)
    main = jnp.zeros((count, LANES), f32)
    tail = None
    for row in range(plan.rows):
        first = plan.width * row
        shift = first - (plan.cut * target - plan.halo)
        rolled = pltpu.roll(pieces[row], shift % LANES, 1)
        low = first + (plan.halo if target == 0 else 0)
        high = first + plan.width - (plan.halo if target == plan.parts - 1 else 0)
        main = jnp.where((lane >= low) & (lane < high), rolled, main)
        if row == plan.rows - 1:
            tail = jnp.where(lane < high - LANES, rolled, 0.0)
    return main, tail


def pack_tail(tail, plan):
    rows = tail.shape[0] // plan.groups
    lane = lane_iota(rows)
    packed = tail[:rows]
    for group in range(1, plan.groups):
        moved = pltpu.roll(tail[rows * group : rows * (group + 1)], plan.tail * group, 1)
        packed = jnp.where(lane >= plan.tail * group, moved, packed)
    return packed


def unpack_tail(packed, plan):
    lane = lane_iota(packed.shape[0])
    parts = [packed]
    for group in range(1, plan.groups):
        parts.append(pltpu.roll(packed, LANES - plan.tail * group, 1))
    return jnp.concatenate([jnp.where(lane < plan.tail, part, 0.0) for part in parts], axis=0)


def first_kernel(plan, conc, cot, cour, direct, rate, orders, stoich, own, columns, *rest):
    sends, pieces = rest[:-1], rest[-1]
    species, rows, parts = plan.species, plan.rows, plan.parts
    flip = lax.axis_index("row") == 1
    me = lax.axis_index("gx")
    order_float = orders[...].astype(f32)
    left = jnp.concatenate([order_float, order_float], axis=1).astype(bf16)
    right = scaled(stoich[...].astype(f32), rate[...])
    stars = []
    half = 2 * LANES
    per = half // LANES
    loaded = [conc[pl.ds(row, species, stride=rows), :] for row in range(rows)]
    for start in range(0, rows, per):
        cells = jnp.concatenate(loaded[start : start + per], axis=1)
        growth = jnp.exp2(mul(left, exponent_input(cells)))
        star = cells + time_step * product(right, growth)
        stars += [star[:, LANES * n : LANES * (n + 1)] for n in range(per)]
    costate = [cot[pl.ds(row, species, stride=rows), :] for row in range(rows)]
    both = [jnp.concatenate([stars[row], costate[row]], axis=0) for row in range(rows)]
    both = [jnp.where(flip, both[rows - 1 - row], both[row]) for row in range(rows)]
    sublane = lax.broadcasted_iota(jnp.int32, (8, LANES), 0)
    facts = []
    for row in range(rows):
        a = jnp.where(flip, cour[rows - 1 - row : rows - row, :], cour[row : row + 1, :])
        b = jnp.where(flip, direct[rows - 1 - row : rows - row, :], direct[row : row + 1, :])
        fact = jnp.where(sublane == 0, a, jnp.where(sublane == 1, b.astype(f32), 1.0))
        facts.append(fact)
    size = 2 * species
    small = size // plan.groups
    for target in range(parts):
        main, tail = window(both, target, plan)
        pieces[target, :size, :] = main
        pieces[target, size : size + small, :] = pack_tail(tail, plan)
        main, tail = window(facts, target, plan)
        pieces[target, size + small : size + small + 8, :] = main
        pieces[target, size + small + 8 : size + small + 16, :] = tail
    own[...] = pieces[me, : size + small, :]
    columns[:, :LANES] = pieces[me, size + small : size + small + 8, :]
    columns[:, LANES:] = pieces[me, size + small + 8 : size + small + 16, :]
    for step, send in enumerate(sends, 1):
        send[...] = pieces[me ^ step, : size + small, :]


def gather_planes(plan, planes, own, received):
    me = lax.axis_index("gx")
    planes[me] = own[...]
    for step, block in enumerate(received, 1):
        planes[me ^ step] = block[...]


def halo_kernel(plan, *refs):
    parts, size = plan.parts, 2 * plan.species
    own, received, columns = refs[0], refs[1:parts], refs[parts]
    inner, outer, planes = refs[parts + 1 :]
    gather_planes(plan, planes, own, received)

    def put(where, count, main, tail):
        outer[where : where + count, :] = main
        lane = lane_iota(count)
        last = (plan.rows - 1) * plan.width
        near = pltpu.roll(main, LANES - last, 1)
        wrapped = pltpu.roll(tail, LANES - last, 1)
        near = jnp.where(lane < LANES - last, near, wrapped)
        far = pltpu.roll(main, (plan.width - last + plan.width) % LANES, 1)
        near = jnp.where(lane < plan.width, near, far)
        inner[where : where + count, :] = near

    small = size // plan.groups
    for plane in range(parts):
        put(plane * size, size, planes[plane, :size, :], unpack_tail(planes[plane, size : size + small, :], plan))
    put(parts * size, 8, columns[:, :LANES], columns[:, LANES:])


def turn(values, amount):
    return pltpu.roll(values, amount % values.shape[1], 1)


def smoothed(values, width):
    beside = turn(values, 1) + turn(values, -1) + turn(values, width) + turn(values, -width)
    return values + diffusion * (beside - 4.0 * values)


def swept(planes, retain, upward):
    count = len(planes)
    rising, falling = [planes[0]], [planes[-1]]
    for n in range(1, count):
        rising.append(retain * rising[-1] + planes[n])
        falling.append(retain * falling[-1] + planes[count - 1 - n])
    falling.reverse()
    return [jnp.where(upward, a, b) for a, b in zip(rising, falling)]


def middle_kernel(plan, *refs):
    parts, species = plan.parts, plan.species
    size = 2 * species
    own, received, columns = refs[0], refs[1:parts], refs[parts]
    inner, outer, left_ref, right_ref, pull_ref, push_ref = refs[parts + 1 : parts + 7]
    results, planes = refs[parts + 7 : -1], refs[-1]
    gather_planes(plan, planes, own, received)
    width, full, part = plan.width, plan.lanes, plan.inner
    small = size // plan.groups

    def whole(main, tail, near, far):
        count = main.shape[0]
        lane = lane_iota(count)
        used = 2 * width
        second = jnp.where((lane >= plan.tail) & (lane < plan.tail + used), pltpu.roll(near, plan.tail, 1), tail)
        last = jnp.where(lane >= LANES - width, pltpu.roll(far, LANES - width, 1), 0.0)
        before = pltpu.roll(far, (LANES - 3 * width) % LANES, 1)
        last = jnp.where((lane >= LANES - 2 * width) & (lane < LANES - width), before, last)
        blocks = [main, second]
        blocks += [jnp.zeros_like(main)] * (full // LANES - 3)
        return jnp.concatenate(blocks + [last], axis=1)

    facts = whole(columns[:, :LANES], columns[:, LANES:], inner[parts * size :, :], outer[parts * size :, :])
    cour = facts[0:1, :]
    admit = 1.0 / (1.0 + cour)
    retain = cour / (1.0 + cour)
    upward = facts[1:2, :] > 0.5
    downward = facts[1:2, :] < 0.5
    inside = facts[2:3, :]

    def cropped(values):
        return turn(values, width)[:, :part]

    states, costates = [], []
    for plane in range(parts):
        rows = slice(plane * size, (plane + 1) * size)
        tail = unpack_tail(planes[plane, size : size + small, :], plan)
        both = whole(planes[plane, :size, :], tail, inner[rows, :], outer[rows, :])
        states.append(admit * smoothed(both[:species], width))
        costates.append(both[species:])
    states = [cropped(v) for v in swept(states, retain, upward)]
    costates = [admit * v for v in swept(costates, retain, downward)]
    costates = [cropped(smoothed(v, width)) for v in costates]
    admit, retain = cropped(admit), cropped(retain)
    inside = cropped(inside) > 0.5
    upward = cropped(facts[1:2, :]) > 0.5
    downward = cropped(facts[1:2, :]) < 0.5
    left, right, pull, push = left_ref[...], right_ref[...], pull_ref[...], push_ref[...]
    stars, backs = [], []
    for plane in range(parts):
        cells, spread = states[plane], costates[plane]
        growth = jnp.exp2(mul(left, exponent_input(cells)))
        star = cells + time_step * product(right, growth)
        stars.append(jnp.where(inside, star, 0.0))
        summed = product(push, growth * mul(pull, stacked(spread)))
        back = spread + time_step * cells / (1.0 + cells * cells) * summed
        backs.append(jnp.where(inside, back, 0.0))
    final = swept([admit * smoothed(v, width) for v in stars], retain, upward)
    spreads = [admit * v for v in swept(backs, retain, downward)]
    spreads = [smoothed(v, width) for v in spreads]

    def dense(values):
        lane = lane_iota(values.shape[0])
        out = None
        for row in range(plan.rows):
            moved = turn(values, plan.cut * row - (width * (row + 1) + plan.halo))[:, :LANES]
            out = moved if row == 0 else jnp.where(lane >= plan.cut * row, moved, out)
        return out

    for plane in range(parts):
        planes[plane, :species, :] = dense(final[plane])
        planes[plane, species:size, :] = dense(spreads[plane])
    me = lax.axis_index("gx")
    for step, result in enumerate(results):
        result[...] = planes[me ^ step, :size, :]


def last_kernel(plan, *refs):
    parts, species, rows = plan.parts, plan.species, plan.rows
    size = 2 * species
    own, received = refs[0], refs[1:parts]
    conc, left_ref, pull_ref, push_ref = refs[parts : parts + 4]
    final, adjoint, planes = refs[parts + 4 :]
    gather_planes(plan, planes, own, received)
    flip = lax.axis_index("row") == 1
    lane = lane_iota(size)
    blocks = []
    for row in range(rows):
        out = None
        for piece in range(parts):
            moved = pltpu.roll(planes[piece, :, :], (plan.cut * (piece - row)) % LANES, 1)
            out = moved if piece == 0 else jnp.where(lane >= plan.cut * piece, moved, out)
        blocks.append(out)
    blocks = [jnp.where(flip, blocks[rows - 1 - row], blocks[row]) for row in range(rows)]
    for row in range(rows):
        final[pl.ds(row, species, stride=rows), :] = blocks[row][:species]
    left, pull, push = left_ref[...], pull_ref[...], push_ref[...]
    per = 2
    for start in range(0, rows, per):
        cells = jnp.concatenate([conc[pl.ds(start + n, species, stride=rows), :] for n in range(per)], axis=1)
        spread = jnp.concatenate([blocks[start + n][species:] for n in range(per)], axis=1)
        growth = jnp.exp2(mul(left, exponent_input(cells)))
        summed = product(push, growth * mul(pull, stacked(spread)))
        back = spread + time_step * cells / (1.0 + cells * cells) * summed
        for n in range(per):
            adjoint[pl.ds(start + n, species, stride=rows), :] = back[:, LANES * n : LANES * (n + 1)]


def tables_kernel(rate, orders, stoich, own, left, right, pull, push):
    order_float = orders[...].astype(f32)
    stoich_float = stoich[...].astype(f32)
    left[...] = jnp.concatenate([order_float, order_float], axis=1).astype(bf16)
    right[...] = scaled(stoich_float, rate[...])
    turned = stoich_float.T
    pull[...] = jnp.concatenate([turned, turned], axis=1).astype(bf16)
    push[...] = scaled(order_float.T, rate[...])


def call(kernel, outs, scratch=(), flops=0):
    return pl.pallas_call(
        kernel,
        out_shape=outs,
        scratch_shapes=scratch,
        compiler_params=pltpu.CompilerParams(vmem_limit_bytes=32 * 1024 * 1024),
        cost_estimate=pl.CostEstimate(flops=flops, bytes_accessed=1 << 20, transcendentals=0),
    )


def columns_path(plan, gy, conc, cotangent, courant, direction, rate_const, orders, stoich):
    species, rows, parts = plan.species, plan.rows, plan.parts
    size = 2 * species
    shape = conc.shape
    count = rate_const.shape[0]
    rate = rate_const.reshape(1, count)
    flat = conc.reshape(species * rows, LANES)
    height = size + size // plan.groups
    block = jax.ShapeDtypeStruct((height, LANES), f32)
    own, columns, *sends = call(
        functools.partial(first_kernel, plan),
        [block, jax.ShapeDtypeStruct((8, 2 * LANES), f32)] + [block] * (parts - 1),
        [pltpu.VMEM((parts, height + 16, LANES), f32)],
        flops=1 << 28,
    )(flat, cotangent.reshape(species * rows, LANES), courant, direction, rate, orders, stoich)
    pairs = [[(i, i ^ step) for i in range(parts)] for step in range(1, parts)]
    received = [lax.ppermute(send, "gx", pair) for send, pair in zip(sends, pairs)]
    left, right, pull, push = call(
        tables_kernel,
        [
            jax.ShapeDtypeStruct((count, size), bf16),
            jax.ShapeDtypeStruct((size, count), bf16),
            jax.ShapeDtypeStruct((count, size), bf16),
            jax.ShapeDtypeStruct((size, count), bf16),
        ],
        flops=1 << 26,
    )(rate, orders, stoich, own)
    planes = pltpu.VMEM((parts, height, LANES), f32)
    edge = jax.ShapeDtypeStruct((parts * size + 8, LANES), f32)
    inner, outer = call(functools.partial(halo_kernel, plan), [edge, edge], [planes], flops=1 << 26)(
        own, *received, columns
    )
    cross = [(2 * n + 1, 2 * n + 2) for n in range(gy - 1)]
    outer = lax.ppermute(outer, ("gy", "row"), cross + [(b, a) for a, b in cross])
    inner = lax.ppermute(inner, "row", [(0, 1), (1, 0)])
    out = jax.ShapeDtypeStruct((size, LANES), f32)
    own, *sends = call(functools.partial(middle_kernel, plan), [out] * parts, [planes], flops=1 << 29)(
        own, *received, columns, inner, outer, left, right, pull, push
    )
    received = [lax.ppermute(send, "gx", pair) for send, pair in zip(sends, pairs)]
    result = jax.ShapeDtypeStruct((species * rows, LANES), f32)
    final, adjoint = call(
        functools.partial(last_kernel, plan),
        [result, result],
        [pltpu.VMEM((parts, size, LANES), f32)],
        flops=1 << 28,
    )(own, *received, flat, left, pull, push)
    return final.reshape(shape), adjoint.reshape(shape)


def solution(mesh):
    placed = (
        P(None, ("grp", "gx"), ("gy", "row"), None),
        P(None, ("grp", "gx"), ("gy", "row"), None),
        P(("grp", "gy", "row"), None),
        P(("grp", "gy", "row"), None),
        P(),
        P(),
        P(),
    )

    def program(*arrays):
        shape = arrays[0].shape
        if fits(mesh, shape):
            rows = shape[2] // (mesh.shape["gy"] * mesh.shape["row"])
            plan = Plan(shape[0], rows, shape[3], mesh.shape["gx"])
            body = functools.partial(columns_path, plan, mesh.shape["gy"])
        else:
            body = general
        return jax.shard_map(
            body,
            mesh=mesh,
            in_specs=placed,
            out_specs=placed[:2],
            check_vma=False,
        )(*arrays)

    return program
```
